256 devices in a mesh: rows: 64 (over x, z_hi, y), feat: 4 (over z_lo, core).
Axes of the slice: x: 4, y: 4, z: 8 (z_hi: 4, z_lo: 2; z = z_hi * 2 + z_lo), core: 2. Of those that a mesh axis runs over, the one named last changes fastest.
Arguments:
- table_cells: bfloat16 [32768, 128, 128], P('rows', 'feat'), may hold values from -6 to 6
- fold_id: int32 [32768], P('rows'), may hold values from 0 to 3, as said below
- train_mask: int32 [32768], P('rows'), may hold values from 0 to 1, as said below
- inducing: bfloat16 [128, 128], replicated, may hold values from -6 to 6
- induce_proj: bfloat16 [128, 256], replicated, may hold values from -0.5 to 0.5
- induce_back: bfloat16 [128, 384], replicated, may hold values from -0.5 to 0.5
- summary_query: bfloat16 [4, 128], replicated, may hold values from -6 to 6
- row_proj: bfloat16 [128, 256], replicated, may hold values from -0.5 to 0.5
- context_proj: bfloat16 [3, 512, 512], P(None, None, 'feat'), may hold values from -0.25 to 0.25
Outputs:
- context: bfloat16 [32768, 512], P('rows', 'feat')
The draws below stay inside these ranges and needn't reach their ends.
Inputs may be any that keep to these rules, and one draw needn't show every extreme that they name: `train_mask`: among the rows of one device (aligned blocks of 512 rows) exactly half are training rows. `fold_id`: among the training rows of each aligned block of 512 rows every fold number occurs.
All inputs are finite; a program needn't handle non-finite values.
Results may differ from the reference program's by a relative error of at most 0.03.
Values may be sent and summed in bfloat16 or wider, within the bound.
No kernel may reach another device: no remote copies, remote signals or barrier semaphores. Data moves between devices by JAX's collectives and lax.ppermute only.
A program may use at most 128 MiB of HBM per device.

```python
import math
import jax
import jax.numpy as jnp
from jax import lax

EMBED = 128
INDUCE = 128
SUMMARY = 4
HEADS = 4
WIDTH = 512
HEAD_DIM = 128
ROWS_DEV = 512
FOLDS = 4
ROWS = 32768
FEATURES = 128


def row_layout(key):
    blocks = ROWS // ROWS_DEV
    block_keys = jax.random.split(jax.random.fold_in(key, 7), blocks)

    def draw_block(block_key):
        key_order, key_folds = jax.random.split(block_key)
        order = jax.random.permutation(key_order, ROWS_DEV)
        spare_folds = jax.random.randint(key_folds, (ROWS_DEV,), 0, FOLDS)
        labelled = (order < ROWS_DEV // 2).astype(jnp.int32)
        folds = jnp.where(order < FOLDS, order, spare_folds).astype(jnp.int32)
        return (labelled, folds)
    labelled, folds = jax.vmap(draw_block)(block_keys)
    return (labelled.reshape(-1), folds.reshape(-1))


def draw_train_mask(key, part):
    return row_layout(key)[0]


def draw_fold_id(key, part):
    return row_layout(key)[1]


def block_scale(key, extent, pieces, low, high):
    def one(position, parts):
        draws = jax.random.uniform(jax.random.fold_in(jax.random.fold_in(key, 6), position), (parts,), jnp.float32, low / len(pieces), high / len(pieces))
        return jnp.repeat(jnp.exp(draws), extent[position] // parts).reshape((-1,) + (1,) * (len(extent) - position - 1))

    loudness = one(*pieces[0])
    for cut in pieces[1:]:
        loudness = loudness * one(*cut)
    return loudness


def centred(own_key, extent, spread, reach, cuts=(), kind=jnp.bfloat16):
    factor_of = block_scale(own_key, extent, cuts, -0.22, 0.18) if cuts else 1.0
    values = jax.random.normal(own_key, extent, jnp.float32) * spread * factor_of
    return jnp.minimum(jnp.maximum(values, -reach), reach).astype(kind)


def setup_inputs(seed: int = 0) -> dict:
    keys = jax.random.split(jax.random.key(seed), 10)
    table_cells = centred(keys[0], (ROWS, FEATURES, EMBED), 1.0, 6.0, ((0, 64), (1, 4)))
    fold_id = draw_fold_id(jax.random.fold_in(keys[9], 71), 0)
    train_mask = draw_train_mask(jax.random.fold_in(keys[9], 71), 0)
    inducing = centred(keys[3], (INDUCE, EMBED), 1.0, 6.0)
    induce_proj = centred(keys[4], (EMBED, 2 * EMBED), EMBED ** -0.5, 0.5)
    induce_back = centred(keys[5], (EMBED, 3 * EMBED), EMBED ** -0.5, 0.5)
    summary_query = centred(keys[6], (SUMMARY, EMBED), 1.0, 6.0)
    row_proj = centred(keys[7], (EMBED, 2 * EMBED), EMBED ** -0.5, 0.5)
    context_proj = centred(keys[8], (3, WIDTH, WIDTH), WIDTH ** -0.5, 0.25, ((2, 4),))
    return {"table_cells": table_cells, "fold_id": fold_id, "train_mask": train_mask, "inducing": inducing, "induce_proj": induce_proj, "induce_back": induce_back, "summary_query": summary_query, "row_proj": row_proj, "context_proj": context_proj}


epsilon = 1e-06
score_scale = 0.25

def rms_normalize(value):
    value = value.astype(jnp.float32)
    return value * lax.rsqrt(lax.optimization_barrier(jnp.mean(value * value, axis=-1, keepdims=True)) + epsilon)

def reference(table_cells, fold_id, train_mask, inducing, induce_proj, induce_back, summary_query, row_proj, context_proj):
    mask_float = train_mask.astype(jnp.float32)
    induce_norm = rms_normalize(inducing).astype(jnp.bfloat16)
    summary_norm = rms_normalize(summary_query).astype(jnp.bfloat16)

    def feature_step(index, totals):
        column = lax.dynamic_slice_in_dim(table_cells, index, 1, 1)[:, 0, :]
        col_kv = jnp.dot(column, induce_proj, preferred_element_type=jnp.float32).astype(jnp.bfloat16)
        col_keys = rms_normalize(col_kv[:, :EMBED]).astype(jnp.bfloat16)
        col_values = col_kv[:, EMBED:]
        scores = jnp.dot(induce_norm, col_keys.T, preferred_element_type=jnp.float32) * score_scale
        weights = (jnp.exp(scores) * mask_float[None, :]).astype(jnp.bfloat16)
        induced = rms_normalize(jnp.dot(weights, col_values, preferred_element_type=jnp.float32)).astype(jnp.bfloat16)
        point_kv = jnp.dot(induced, induce_back[:, EMBED:], preferred_element_type=jnp.float32).astype(jnp.bfloat16)
        cell_query = jnp.dot(column, induce_back[:, :EMBED], preferred_element_type=jnp.float32).astype(jnp.bfloat16)
        query_norm = rms_normalize(cell_query).astype(jnp.bfloat16)
        point_keys = rms_normalize(point_kv[:, :EMBED]).astype(jnp.bfloat16)
        cell_scores = jnp.dot(query_norm, point_keys.T, preferred_element_type=jnp.float32) * score_scale
        expos = jnp.exp(cell_scores)
        probs = (expos / lax.optimization_barrier(jnp.sum(expos, axis=-1, keepdims=True))).astype(jnp.bfloat16)
        attended = jnp.dot(probs, point_kv[:, EMBED:], preferred_element_type=jnp.float32)
        updated = (column.astype(jnp.float32) + attended).astype(jnp.bfloat16)
        row_kv = jnp.dot(updated, row_proj, preferred_element_type=jnp.float32).astype(jnp.bfloat16)
        row_keys = rms_normalize(row_kv[:, :EMBED]).astype(jnp.bfloat16)
        summary_weights = jnp.exp(jnp.dot(row_keys, summary_norm.T, preferred_element_type=jnp.float32) * score_scale).astype(jnp.bfloat16)
        return totals + summary_weights.astype(jnp.float32)[:, :, None] * row_kv[:, None, EMBED:].astype(jnp.float32)
    totals = lax.fori_loop(0, FEATURES, feature_step, jnp.zeros((ROWS, SUMMARY, EMBED), jnp.float32))
    represent = rms_normalize(totals).astype(jnp.bfloat16).reshape(ROWS, WIDTH)
    projected = [jnp.dot(represent, context_proj[which], preferred_element_type=jnp.float32).astype(jnp.bfloat16) for which in range(3)]
    query_heads = rms_normalize(projected[0].reshape(ROWS, HEADS, HEAD_DIM)).astype(jnp.bfloat16)
    key_heads = rms_normalize(projected[1].reshape(ROWS, HEADS, HEAD_DIM)).astype(jnp.bfloat16)
    value_heads = projected[2].reshape(ROWS, HEADS, HEAD_DIM)
    chosen = jnp.argsort(1 - train_mask, stable=True)[:ROWS // 2].astype(jnp.int32)
    train_keys = key_heads[chosen].astype(jnp.float32)
    train_values = value_heads[chosen].astype(jnp.float32)
    train_folds = fold_id[chosen]
    block = math.gcd(ROWS, 512)

    def query_block(index):
        start = (index * block).astype(jnp.int32)
        queries = lax.dynamic_slice_in_dim(query_heads, start, block, 0).astype(jnp.float32)
        folds = lax.dynamic_slice_in_dim(fold_id, start, block, 0)
        scores = jnp.einsum('qhd,khd->hqk', queries, train_keys) * score_scale
        allow = (train_folds[None, :] != folds[:, None]).astype(jnp.float32)
        weights = (jnp.exp(scores) * allow[None]).astype(jnp.bfloat16)
        summed = jnp.einsum('hqk,khd->qhd', weights.astype(jnp.float32), train_values)
        return rms_normalize(summed).astype(jnp.bfloat16).reshape(block, WIDTH)
    outputs = lax.map(query_block, jnp.arange(ROWS // block, dtype=jnp.int32))
    return outputs.reshape(ROWS, WIDTH)
```

```python
import jax
import jax.numpy as jnp
from jax import lax
from jax.experimental import pallas as pl
from jax.experimental.pallas import tpu as pltpu
from jax.sharding import Mesh, PartitionSpec as P

HEAD_DIM = 128
XY = ("x", "y")
FEAT = ("zl", "core")
KEY_GROUP = ("x", "y", "zl", "core")
QUERY_GROUP = ("zh", "zl", "core")

epsilon = 1e-06
score_scale = 0.25
LOG2E = 1.4426950408889634
FOLD_PENALTY = 16384.0


def rms_normalize(value):
    value = value.astype(jnp.float32)
    return value * lax.rsqrt(jnp.mean(value * value, axis=-1, keepdims=True) + epsilon)


def exchange(value, axes):
    return lax.all_to_all(value, axes, 0, 0, tiled=True)


def attention_kernel(q_ref, k_ref, v_ref, o_ref, *, key_block):
    q = q_ref[...]
    total = jnp.zeros(o_ref.shape, jnp.float32)
    for start in range(0, k_ref.shape[0], key_block):
        scores = lax.dot_general(
            q,
            k_ref[start : start + key_block, :],
            (((1,), (1,)), ((), ())),
            preferred_element_type=jnp.float32,
        )
        weights = jnp.exp2(scores).astype(jnp.bfloat16)
        total = total + jnp.dot(
            weights, v_ref[start : start + key_block, :], preferred_element_type=jnp.float32
        )
    o_ref[...] = total.astype(o_ref.dtype)


def attention(q, k, v, query_block=512, key_block=512):
    queries, width = q.shape
    keys = k.shape[0]
    return pl.pallas_call(
        lambda *refs: attention_kernel(*refs, key_block=key_block),
        out_shape=jax.ShapeDtypeStruct((queries, HEAD_DIM), jnp.bfloat16),
        grid=(queries // query_block,),
        in_specs=[
            pl.BlockSpec((query_block, width), lambda i: (i, 0)),
            pl.BlockSpec((keys, width), lambda i: (0, 0)),
            pl.BlockSpec((keys, HEAD_DIM), lambda i: (0, 0)),
        ],
        out_specs=pl.BlockSpec((query_block, HEAD_DIM), lambda i: (i, 0)),
        name="attention",
    )(q, k, v)


def other(value, axis):
    return lax.ppermute(value, axis, [(0, 1), (1, 0)])


def local(
    table_cells,
    fold_id,
    train_mask,
    inducing,
    induce_proj,
    induce_back,
    summary_query,
    row_proj,
    context_proj,
):
    rows_here, feats_here, embed = table_cells.shape
    width = context_proj.shape[1]
    zl = lax.axis_index("zl")
    core = lax.axis_index("core")
    zh = lax.axis_index("zh")
    xy = lax.axis_index("x") * lax.axis_size("y") + lax.axis_index("y")
    groups_xy = lax.axis_size("x") * lax.axis_size("y")
    groups_z = lax.axis_size("zh")
    feat_devices = lax.axis_size("zl") * lax.axis_size("core")
    block = rows_here // feat_devices
    half = block // 2

    proj_pair = jnp.concatenate([context_proj, other(context_proj, "core")], axis=2)
    proj_full = jnp.concatenate([proj_pair, other(proj_pair, "zl")], axis=2)

    labelled = (train_mask == 1).astype(jnp.bfloat16)
    index = jnp.arange(rows_here)
    before = (index[:, None] < index[None, :]).astype(jnp.bfloat16)
    rank_train = jnp.dot(labelled[None], before, preferred_element_type=jnp.float32)[0].astype(
        jnp.int32
    )
    rank = jnp.where(train_mask == 1, rank_train, index - rank_train)
    slot = (rank // half) * block + rank % half + jnp.where(train_mask == 1, 0, half)
    permute = (index[:, None] == slot[None, :]).astype(jnp.bfloat16)
    codes = jnp.dot(
        permute, fold_id.astype(jnp.bfloat16)[:, None], preferred_element_type=jnp.float32
    ).astype(jnp.bfloat16)
    codes = codes.reshape(feat_devices, block)

    col_kv = jnp.einsum(
        "rfe,ek->rfk", table_cells, induce_proj, preferred_element_type=jnp.float32
    ).astype(jnp.bfloat16)
    col_keys = rms_normalize(col_kv[..., :embed]).astype(jnp.bfloat16)
    col_values = col_kv[..., embed:]
    induce_norm = rms_normalize(inducing).astype(jnp.bfloat16)
    scores = (
        jnp.einsum("me,rfe->fmr", induce_norm, col_keys, preferred_element_type=jnp.float32)
        * score_scale
    )
    weights = (jnp.exp(scores) * train_mask.astype(jnp.float32)).astype(jnp.bfloat16)
    numerator = jnp.einsum(
        "fmr,rfe->fme", weights, col_values, preferred_element_type=jnp.float32
    ).astype(jnp.bfloat16)

    points = inducing.shape[0]
    share_xy = feats_here * points // groups_xy
    share = share_xy // groups_z
    part = exchange(numerator.reshape(groups_xy, share_xy, embed), XY)
    part = jnp.sum(part.astype(jnp.float32), axis=0).astype(jnp.bfloat16)
    part = exchange(part.reshape(groups_z, share, embed), "zh")
    mine = rms_normalize(jnp.sum(part.astype(jnp.float32), axis=0)).astype(jnp.bfloat16)
    sent = jnp.concatenate([mine, jnp.pad(codes, ((0, 12), (0, 0)))], axis=0)
    got = exchange(jnp.broadcast_to(sent[None], (groups_z,) + sent.shape), "zh")
    sent = jnp.concatenate(
        [got[:, :share].reshape(share_xy, embed), got[:, share : share + 4].reshape(-1, embed)],
        axis=0,
    )
    got = exchange(jnp.broadcast_to(sent[None], (groups_xy,) + sent.shape), XY)
    induced = got[:, :share_xy].reshape(feats_here, points, embed)
    all_codes = got[:, share_xy:].reshape(groups_xy, groups_z, feat_devices, block)

    point_kv = jnp.einsum(
        "fme,ek->fmk", induced, induce_back[:, embed:], preferred_element_type=jnp.float32
    ).astype(jnp.bfloat16)
    cell_query = jnp.einsum(
        "rfe,ek->rfk", table_cells, induce_back[:, :embed], preferred_element_type=jnp.float32
    ).astype(jnp.bfloat16)
    query_norm = rms_normalize(cell_query).astype(jnp.bfloat16)
    point_keys = rms_normalize(point_kv[..., :embed]).astype(jnp.bfloat16)
    cell_scores = (
        jnp.einsum("rfe,fme->rfm", query_norm, point_keys, preferred_element_type=jnp.float32)
        * score_scale
    )
    expos = jnp.exp(cell_scores)
    probs = (expos / jnp.sum(expos, axis=-1, keepdims=True)).astype(jnp.bfloat16)
    attended = jnp.einsum(
        "rfm,fme->rfe", probs, point_kv[..., embed:], preferred_element_type=jnp.float32
    )
    updated = (table_cells.astype(jnp.float32) + attended).astype(jnp.bfloat16)
    row_kv = jnp.einsum(
        "rfe,ek->rfk", updated, row_proj, preferred_element_type=jnp.float32
    ).astype(jnp.bfloat16)
    row_keys = rms_normalize(row_kv[..., :embed]).astype(jnp.bfloat16)
    summary_norm = rms_normalize(summary_query).astype(jnp.bfloat16)
    summary_scores = (
        jnp.einsum("ce,rfe->rcf", summary_norm, row_keys, preferred_element_type=jnp.float32)
        * score_scale
    )
    summary_weights = jnp.exp(summary_scores).astype(jnp.bfloat16)
    partial_value = jnp.einsum(
        "rcf,rfe->rce", summary_weights, row_kv[..., embed:], preferred_element_type=jnp.float32
    ).astype(jnp.bfloat16)

    ordered = jnp.dot(
        permute, partial_value.reshape(rows_here, width), preferred_element_type=jnp.float32
    ).astype(jnp.bfloat16)
    got = exchange(ordered.reshape(feat_devices, block, width), FEAT)
    totals = jnp.sum(got.astype(jnp.float32), axis=0)
    represent = rms_normalize(totals.reshape(block, -1, embed)).astype(jnp.bfloat16)
    projected = jnp.einsum(
        "rd,kdc->krc",
        represent.reshape(block, width),
        proj_full,
        preferred_element_type=jnp.float32,
    ).astype(jnp.bfloat16)

    def heads(value):
        value = value.reshape(-1, 2, 2, HEAD_DIM).transpose(1, 2, 0, 3)
        value = jnp.where(zl == 0, value, value[::-1])
        return jnp.where(core == 0, value, value[:, ::-1]).reshape(
            feat_devices, -1, HEAD_DIM
        )

    q = (rms_normalize(heads(projected[0])) * (score_scale * LOG2E)).astype(jnp.bfloat16)
    k = rms_normalize(heads(projected[1][:half])).astype(jnp.bfloat16)
    v = heads(projected[2][:half])
    q_all = exchange(
        jnp.broadcast_to(q[None], (groups_z,) + q.shape).reshape(-1, block, HEAD_DIM), QUERY_GROUP
    ).reshape(-1, HEAD_DIM)
    kv = jnp.concatenate([k, v], axis=1)
    kv_all = exchange(
        jnp.broadcast_to(kv[None], (groups_xy,) + kv.shape).reshape(-1, 2 * half, HEAD_DIM),
        KEY_GROUP,
    )
    k_all = kv_all[:, :half].reshape(-1, HEAD_DIM)
    v_all = kv_all[:, half:].reshape(-1, HEAD_DIM)
    query_codes = lax.dynamic_index_in_dim(all_codes, xy, 0, keepdims=False).reshape(-1)
    key_codes = lax.dynamic_index_in_dim(all_codes, zh, 1, keepdims=False)[..., :half].reshape(-1)
    lanes = jnp.arange(HEAD_DIM).astype(jnp.float32)
    query_marks = jnp.where(
        query_codes.astype(jnp.float32)[:, None] == lanes[None], -FOLD_PENALTY, 0.0
    ).astype(jnp.bfloat16)
    key_marks = (key_codes.astype(jnp.float32)[:, None] == lanes[None]).astype(jnp.bfloat16)
    summed = attention(
        jnp.concatenate([q_all, query_marks], axis=1),
        jnp.concatenate([k_all, key_marks], axis=1),
        v_all,
    )
    got = exchange(summed.reshape(groups_z, rows_here, HEAD_DIM), "zh")
    context = rms_normalize(jnp.sum(got.astype(jnp.float32), axis=0)).astype(jnp.bfloat16)
    return lax.dot_general(
        permute, context, (((0,), (0,)), ((), ())), preferred_element_type=jnp.float32
    ).astype(jnp.bfloat16)


def solution(mesh):
    fine = Mesh(mesh.devices.reshape(4, 4, 4, 2, 2), ("x", "zh", "y", "zl", "core"))
    rows = ("x", "zh", "y")
    in_specs = (
        P(rows, FEAT, None),
        P(rows),
        P(rows),
        P(),
        P(),
        P(),
        P(),
        P(),
        P(None, None, FEAT),
    )
    return jax.shard_map(
        local, mesh=fine, in_specs=in_specs, out_specs=P(rows, FEAT), check_vma=False
    )
```

```python
import jax
import jax.numpy as jnp
from jax import lax
from jax.experimental import pallas as pl
from jax.experimental.pallas import tpu as pltpu
from jax.sharding import Mesh, PartitionSpec as P

HEAD_DIM = 128
XY = ("x", "y")
FEAT = ("zl", "core")
KEY_GROUP = ("x", "y", "zl", "core")
QUERY_GROUP = ("zh", "zl", "core")
FOLD_PENALTY = 16384.0

epsilon = 1e-06
score_scale = 0.25
LOG2E = 1.4426950408889634
EXCLUDED = -1e9


def rms_normalize(value):
    value = value.astype(jnp.float32)
    return value * lax.rsqrt(jnp.mean(value * value, axis=-1, keepdims=True) + epsilon)


def product(a, b):
    return jnp.dot(a, b, preferred_element_type=jnp.float32)


def product_nt(a, b):
    return lax.dot_general(a, b, (((1,), (1,)), ((), ())), preferred_element_type=jnp.float32)


def induce_kernel(x_ref, bias_ref, proj_ref, points_ref, cells_ref, sums_ref, stage_ref):
    chunk, feats, embed = x_ref.shape
    step = pl.program_id(0)
    stage_ref[...] = x_ref[...].astype(jnp.float32).reshape(chunk * feats, embed)
    first = pl.multiple_of(step * chunk, chunk)
    for f in range(feats):
        cells_ref[f, pl.ds(first, chunk), :] = stage_ref[
            pl.ds(f, chunk, stride=feats), :
        ].astype(jnp.bfloat16)

    @pl.when(step == pl.num_programs(0) - 1)
    def _():
        points = points_ref[...]
        ones = jnp.ones((8, embed), jnp.bfloat16)
        bias = bias_ref[0:1, :]

        def feature(f, carry):
            kv = product(cells_ref[f], proj_ref[...]).astype(jnp.bfloat16)
            keys = kv[:, :embed]
            wide = keys.astype(jnp.float32)
            squares = product_nt(ones, (wide * wide).astype(jnp.bfloat16))
            factor = lax.rsqrt(squares * (1.0 / embed) + epsilon) * (score_scale * LOG2E)
            scores = product_nt(points, keys) * factor[0:1, :] + bias
            weights = jnp.exp2(scores).astype(jnp.bfloat16)
            sums_ref[f] = product(weights, kv[:, embed:]).astype(jnp.bfloat16)
            return carry

        lax.fori_loop(0, feats, feature, 0, unroll=4)


def induce(table_cells, bias, induce_proj, induce_norm, chunk=64):
    rows, feats, embed = table_cells.shape
    points = induce_norm.shape[0]
    return pl.pallas_call(
        induce_kernel,
        out_shape=(
            jax.ShapeDtypeStruct((feats, rows, embed), jnp.bfloat16),
            jax.ShapeDtypeStruct((feats, points, embed), jnp.bfloat16),
        ),
        grid=(rows // chunk,),
        in_specs=[
            pl.BlockSpec((chunk, feats, embed), lambda i: (i, 0, 0)),
            pl.BlockSpec(bias.shape, lambda i: (0, 0)),
            pl.BlockSpec(induce_proj.shape, lambda i: (0, 0)),
            pl.BlockSpec(induce_norm.shape, lambda i: (0, 0)),
        ],
        out_specs=(
            pl.BlockSpec((feats, rows, embed), lambda i: (0, 0, 0)),
            pl.BlockSpec((feats, points, embed), lambda i: (0, 0, 0)),
        ),
        scratch_shapes=[pltpu.VMEM((chunk * feats, embed), jnp.float32)],
        name="induce",
    )(table_cells, bias, induce_proj, induce_norm)


def cell_query_kernel(x_ref, proj_ref, o_ref):
    feats, rows, embed = x_ref.shape
    query = product(x_ref[...].reshape(feats * rows, embed), proj_ref[...]).astype(jnp.bfloat16)
    o_ref[...] = rms_normalize(query).astype(jnp.bfloat16).reshape(o_ref.shape)


def cell_queries(cells, proj, step=4):
    feats, rows, embed = cells.shape
    return pl.pallas_call(
        cell_query_kernel,
        out_shape=jax.ShapeDtypeStruct(cells.shape, jnp.bfloat16),
        grid=(feats // step,),
        in_specs=[
            pl.BlockSpec((step, rows, embed), lambda i: (i, 0, 0)),
            pl.BlockSpec(proj.shape, lambda i: (0, 0)),
        ],
        out_specs=pl.BlockSpec((step, rows, embed), lambda i: (i, 0, 0)),
        name="cell_queries",
    )(cells, proj)


def summary_kernel(
    induced_ref, cells_ref, query_ref, back_ref, row_ref, summary_ref, permute_ref, o_ref, total_ref
):
    step = pl.program_id(0)
    feats, rows, embed = cells_ref.shape
    points = embed
    summaries = total_ref.shape[1] // embed
    back = back_ref[...]
    row_proj = row_ref[...]
    summary = summary_ref[...]
    ones = jnp.ones((points, embed), jnp.bfloat16)
    parts = []
    for f in range(feats):
        induced = induced_ref[0, f * points : (f + 1) * points, :]
        point_kv = product(induced, back).astype(jnp.bfloat16)
        point_keys = (rms_normalize(point_kv[:, :embed]) * (score_scale * LOG2E)).astype(
            jnp.bfloat16
        )
        expos = jnp.exp2(product_nt(query_ref[f], point_keys)).astype(jnp.bfloat16)
        mixed = product(expos, jnp.concatenate([point_kv[:, embed:], ones], axis=1))
        attended = mixed[:, :embed] / mixed[:, embed:]
        updated = (cells_ref[f].astype(jnp.float32) + attended).astype(jnp.bfloat16)
        row_kv = product(updated, row_proj).astype(jnp.bfloat16)
        keys = row_kv[:, :embed]
        wide = keys.astype(jnp.float32)
        factor = lax.rsqrt(jnp.mean(wide * wide, axis=-1, keepdims=True) + epsilon)
        weights = jnp.exp2(product(keys, summary) * (factor * (score_scale * LOG2E)))
        parts.append(
            (weights.astype(jnp.bfloat16).astype(jnp.float32), row_kv[:, embed:].astype(jnp.float32))
        )
    for c in range(summaries):
        addend = parts[0][0][:, c : c + 1] * parts[0][1]
        for weights, values in parts[1:]:
            addend = addend + weights[:, c : c + 1] * values
        span = slice(c * embed, (c + 1) * embed)

        @pl.when(step == 0)
        def _():
            total_ref[:, span] = addend

        @pl.when(step > 0)
        def _():
            total_ref[:, span] += addend

    @pl.when(step == pl.num_programs(0) - 1)
    def _():
        o_ref[...] = product(permute_ref[...], total_ref[...].astype(jnp.bfloat16)).astype(
            jnp.bfloat16
        )


def summarize(induced, cells, queries, back, row_proj, summary, permute, summaries, step=2):
    feats, rows, embed = cells.shape
    width = summaries * embed
    return pl.pallas_call(
        summary_kernel,
        out_shape=jax.ShapeDtypeStruct((rows, width), jnp.bfloat16),
        grid=(feats // step,),
        in_specs=[
            pl.BlockSpec((1,) + induced.shape[1:], lambda i: (i, 0, 0)),
            pl.BlockSpec((step, rows, embed), lambda i: (i, 0, 0)),
            pl.BlockSpec((step, rows, embed), lambda i: (i, 0, 0)),
            pl.BlockSpec(back.shape, lambda i: (0, 0)),
            pl.BlockSpec(row_proj.shape, lambda i: (0, 0)),
            pl.BlockSpec(summary.shape, lambda i: (0, 0)),
            pl.BlockSpec(permute.shape, lambda i: (0, 0)),
        ],
        out_specs=pl.BlockSpec((rows, width), lambda i: (0, 0)),
        scratch_shapes=[pltpu.VMEM((rows, width), jnp.float32)],
        name="summarize",
    )(induced, cells, queries, back, row_proj, summary, permute)


def attention_kernel(q_ref, qm_ref, kv_ref, km_ref, o_ref, *, groups):
    q = jnp.concatenate([q_ref[...], qm_ref[...]], axis=1)
    count, both, dim = kv_ref.shape
    half = both // 2
    total = jnp.zeros(o_ref.shape, jnp.float32)
    for g in range(0, count, groups):
        k = jnp.concatenate(
            [
                kv_ref[g : g + groups, :half, :].reshape(groups * half, dim),
                km_ref[g * half : (g + groups) * half, :],
            ],
            axis=1,
        )
        v = kv_ref[g : g + groups, half:, :].reshape(groups * half, dim)
        weights = jnp.exp2(product_nt(q, k)).astype(jnp.bfloat16)
        total = total + product(weights, v)
    o_ref[...] = total.astype(o_ref.dtype)


def attention(q, q_marks, kv, k_marks, query_block=512, groups=8):
    queries, dim = q.shape
    return pl.pallas_call(
        lambda *refs: attention_kernel(*refs, groups=groups),
        out_shape=jax.ShapeDtypeStruct((queries, dim), jnp.bfloat16),
        grid=(queries // query_block,),
        in_specs=[
            pl.BlockSpec((query_block, dim), lambda i: (i, 0)),
            pl.BlockSpec((query_block, dim), lambda i: (i, 0)),
            pl.BlockSpec(kv.shape, lambda i: (0, 0, 0)),
            pl.BlockSpec(k_marks.shape, lambda i: (0, 0)),
        ],
        out_specs=pl.BlockSpec((query_block, dim), lambda i: (i, 0)),
        name="attention",
    )(q, q_marks, kv, k_marks)

def exchange(value, axes):
    return lax.all_to_all(value, axes, 0, 0, tiled=True)


def other(value, axis):
    return lax.ppermute(value, axis, [(0, 1), (1, 0)])


def local(
    table_cells,
    fold_id,
    train_mask,
    inducing,
    induce_proj,
    induce_back,
    summary_query,
    row_proj,
    context_proj,
):
    rows_here, feats_here, embed = table_cells.shape
    width = context_proj.shape[1]
    zl = lax.axis_index("zl")
    core = lax.axis_index("core")
    zh = lax.axis_index("zh")
    xy = lax.axis_index("x") * lax.axis_size("y") + lax.axis_index("y")
    groups_xy = lax.axis_size("x") * lax.axis_size("y")
    groups_z = lax.axis_size("zh")
    feat_devices = lax.axis_size("zl") * lax.axis_size("core")
    block = rows_here // feat_devices
    half = block // 2

    proj_pair = jnp.concatenate([context_proj, other(context_proj, "core")], axis=2)
    proj_full = jnp.concatenate([proj_pair, other(proj_pair, "zl")], axis=2)

    labelled = (train_mask == 1).astype(jnp.bfloat16)
    index = jnp.arange(rows_here)
    before = (index[:, None] < index[None, :]).astype(jnp.bfloat16)
    rank_train = jnp.dot(labelled[None], before, preferred_element_type=jnp.float32)[0].astype(
        jnp.int32
    )
    rank = jnp.where(train_mask == 1, rank_train, index - rank_train)
    slot = (rank // half) * block + rank % half + jnp.where(train_mask == 1, 0, half)
    permute = (index[:, None] == slot[None, :]).astype(jnp.bfloat16)
    codes = jnp.dot(
        permute, fold_id.astype(jnp.bfloat16)[:, None], preferred_element_type=jnp.float32
    ).astype(jnp.bfloat16)
    codes = codes.reshape(feat_devices, block)

    induce_norm = rms_normalize(inducing).astype(jnp.bfloat16)
    bias = jnp.broadcast_to(
        jnp.where(train_mask == 1, 0.0, EXCLUDED)[None], (8, rows_here)
    ).astype(jnp.float32)
    cells, numerator = induce(table_cells, bias, induce_proj, induce_norm)
    points = inducing.shape[0]
    share_xy = feats_here * points // groups_xy
    part = exchange(numerator.reshape(groups_xy, share_xy, embed), XY)
    part, proj_full = lax.optimization_barrier((part, proj_full))
    part = jnp.sum(part.astype(jnp.float32), axis=0).astype(jnp.bfloat16)
    queries = cell_queries(cells, induce_back[:, :embed])
    sent = jnp.concatenate([part, jnp.pad(codes, ((0, 12), (0, 0)))], axis=0)
    got = exchange(jnp.broadcast_to(sent[None], (groups_z,) + sent.shape), "zh")
    mine = rms_normalize(jnp.sum(got[:, :share_xy].astype(jnp.float32), axis=0))
    sent = jnp.concatenate(
        [mine.astype(jnp.bfloat16), got[:, share_xy : share_xy + 4].reshape(-1, embed)], axis=0
    )
    got = exchange(jnp.broadcast_to(sent[None], (groups_xy,) + sent.shape), XY)
    all_codes = got[:, share_xy:].reshape(groups_xy, groups_z, feat_devices, block)

    summary = rms_normalize(summary_query).astype(jnp.bfloat16).T
    summaries = summary.shape[1]
    summary = jnp.pad(summary, ((0, 0), (0, embed - summaries)))
    ordered = summarize(
        got, cells, queries, induce_back[:, embed:], row_proj, summary, permute, summaries
    )
    got = exchange(ordered.reshape(feat_devices, block, width), FEAT)
    totals = jnp.sum(got.astype(jnp.float32), axis=0)
    represent = rms_normalize(totals.reshape(block, -1, embed)).astype(jnp.bfloat16)
    projected = jnp.einsum(
        "rd,kdc->krc",
        represent.reshape(block, width),
        proj_full,
        preferred_element_type=jnp.float32,
    ).astype(jnp.bfloat16)

    def heads(value):
        value = value.reshape(-1, 2, 2, HEAD_DIM).transpose(1, 2, 0, 3)
        value = jnp.where(zl == 0, value, value[::-1])
        return jnp.where(core == 0, value, value[:, ::-1]).reshape(
            feat_devices, -1, HEAD_DIM
        )

    q = (rms_normalize(heads(projected[0])) * (score_scale * LOG2E)).astype(jnp.bfloat16)
    k = rms_normalize(heads(projected[1][:half])).astype(jnp.bfloat16)
    v = heads(projected[2][:half])
    q_all = exchange(
        jnp.broadcast_to(q[None], (groups_z,) + q.shape).reshape(-1, block, HEAD_DIM), QUERY_GROUP
    ).reshape(-1, HEAD_DIM)
    kv = jnp.concatenate([k, v], axis=1)
    kv_all = exchange(
        jnp.broadcast_to(kv[None], (groups_xy,) + kv.shape).reshape(-1, 2 * half, HEAD_DIM),
        KEY_GROUP,
    )
    query_codes = lax.dynamic_index_in_dim(all_codes, xy, 0, keepdims=False).reshape(-1)
    key_codes = lax.dynamic_index_in_dim(all_codes, zh, 1, keepdims=False)[..., :half].reshape(-1)
    lanes = jnp.arange(HEAD_DIM).astype(jnp.float32)
    query_marks = jnp.where(
        query_codes.astype(jnp.float32)[:, None] == lanes[None], -FOLD_PENALTY, 0.0
    ).astype(jnp.bfloat16)
    key_marks = (key_codes.astype(jnp.float32)[:, None] == lanes[None]).astype(jnp.bfloat16)
    summed = attention(q_all, query_marks, kv_all, key_marks)
    got = exchange(summed.reshape(groups_z, rows_here, HEAD_DIM), "zh")
    context = rms_normalize(jnp.sum(got.astype(jnp.float32), axis=0)).astype(jnp.bfloat16)
    return lax.dot_general(
        permute, context, (((0,), (0,)), ((), ())), preferred_element_type=jnp.float32
    ).astype(jnp.bfloat16)


def solution(mesh):
    fine = Mesh(mesh.devices.reshape(4, 4, 4, 2, 2), ("x", "zh", "y", "zl", "core"))
    rows = ("x", "zh", "y")
    in_specs = (
        P(rows, FEAT, None),
        P(rows),
        P(rows),
        P(),
        P(),
        P(),
        P(),
        P(),
        P(None, None, FEAT),
    )
    return jax.shard_map(
        local, mesh=fine, in_specs=in_specs, out_specs=P(rows, FEAT), check_vma=False
    )
```

```python
import jax
import jax.numpy as jnp
from jax import lax
from jax.experimental import pallas as pl
from jax.experimental.pallas import tpu as pltpu
from jax.sharding import Mesh, PartitionSpec as P

HEAD_DIM = 128
XY = ("x", "y")
FEAT = ("zl", "core")
KEY_GROUP = ("x", "y", "zl", "core")
FOLD_PENALTY = 16384.0

epsilon = 1e-06
score_scale = 0.25
LOG2E = 1.4426950408889634
EXCLUDED = -1e9


def rms_normalize(value):
    value = value.astype(jnp.float32)
    return value * lax.rsqrt(jnp.mean(value * value, axis=-1, keepdims=True) + epsilon)


def product(a, b):
    return jnp.dot(a, b, preferred_element_type=jnp.float32)


def product_nt(a, b):
    return lax.dot_general(a, b, (((1,), (1,)), ((), ())), preferred_element_type=jnp.float32)


def induce_kernel(
    x_ref, bias_ref, proj_ref, points_ref, order_ref, cells_ref, sums_ref, kv_ref, values_ref, weights_ref
):
    chunk, feats, embed = x_ref.shape
    step = pl.program_id(0)
    first = pl.multiple_of(step * chunk, chunk)
    order = order_ref[...]
    for r in range(0, chunk, 16):
        low = x_ref[r : r + 8].reshape(8 * feats, embed)
        high = x_ref[r + 8 : r + 16].reshape(8 * feats, embed)
        moved = product(order, jnp.concatenate([low, high], axis=1))
        low = moved[:, :embed].reshape(feats, 8, embed)
        high = moved[:, embed:].reshape(feats, 8, embed)
        cells_ref[:, pl.ds(first + r, 16), :] = jnp.concatenate([low, high], axis=1).astype(
            jnp.bfloat16
        )

    @pl.when(step == pl.num_programs(0) - 1)
    def _():
        points = points_ref[...]
        bias = bias_ref[0:1, :]
        pair = 4

        def project(f, slot):
            kv_ref[slot] = product(cells_ref[f], proj_ref[...]).astype(jnp.bfloat16)

        def weigh(slot):
            keys = kv_ref[slot, :, :embed].astype(jnp.float32)
            factor = lax.rsqrt(jnp.mean(keys * keys, axis=-1, keepdims=True) + epsilon)
            keys = (keys * (factor * (score_scale * LOG2E))).astype(jnp.bfloat16)
            values_ref[slot] = kv_ref[slot, :, embed:]
            weights_ref[slot] = jnp.exp2(product_nt(points, keys) + bias).astype(jnp.bfloat16)

        def add_up(f, slot):
            sums_ref[f] = product(weights_ref[slot], values_ref[slot]).astype(jnp.bfloat16)

        def features(i, carry):
            for j in range(pair):
                ahead = jnp.minimum(i * pair + j + 1, feats - 1)
                add_up(jnp.maximum(i * pair + j - 1, 0), 1 - j % 2)
                project(ahead, 1 - j % 2)
                weigh(j % 2)
            return carry

        project(0, 0)
        lax.fori_loop(0, feats // pair, features, 0)
        add_up(feats - 1, 1)


def induce(table_cells, bias, induce_proj, induce_norm, chunk=64):
    rows, feats, embed = table_cells.shape
    points = induce_norm.shape[0]
    place = jnp.arange(8 * feats)
    order = ((place[:, None] % 8) * feats + place[:, None] // 8 == place[None, :]).astype(
        jnp.bfloat16
    )
    return pl.pallas_call(
        induce_kernel,
        out_shape=(
            jax.ShapeDtypeStruct((feats, rows, embed), jnp.bfloat16),
            jax.ShapeDtypeStruct((feats, points, embed), jnp.bfloat16),
        ),
        grid=(rows // chunk,),
        in_specs=[
            pl.BlockSpec((chunk, feats, embed), lambda i: (i, 0, 0)),
            pl.BlockSpec(bias.shape, lambda i: (0, 0)),
            pl.BlockSpec(induce_proj.shape, lambda i: (0, 0)),
            pl.BlockSpec(induce_norm.shape, lambda i: (0, 0)),
            pl.BlockSpec(order.shape, lambda i: (0, 0)),
        ],
        out_specs=(
            pl.BlockSpec((feats, rows, embed), lambda i: (0, 0, 0)),
            pl.BlockSpec((feats, points, embed), lambda i: (0, 0, 0)),
        ),
        scratch_shapes=[
            pltpu.VMEM((2, rows, 2 * embed), jnp.bfloat16),
            pltpu.VMEM((2, rows, embed), jnp.bfloat16),
            pltpu.VMEM((2, points, rows), jnp.bfloat16),
        ],
        name="induce",
    )(table_cells, bias, induce_proj, induce_norm, order)


def cell_query_kernel(x_ref, proj_ref, o_ref):
    feats, rows, embed = x_ref.shape
    query = product(x_ref[...].reshape(feats * rows, embed), proj_ref[...]).astype(jnp.bfloat16)
    o_ref[...] = rms_normalize(query).astype(jnp.bfloat16).reshape(o_ref.shape)


def cell_queries(cells, proj, step=4):
    feats, rows, embed = cells.shape
    return pl.pallas_call(
        cell_query_kernel,
        out_shape=jax.ShapeDtypeStruct(cells.shape, jnp.bfloat16),
        grid=(feats // step,),
        in_specs=[
            pl.BlockSpec((step, rows, embed), lambda i: (i, 0, 0)),
            pl.BlockSpec(proj.shape, lambda i: (0, 0)),
        ],
        out_specs=pl.BlockSpec((step, rows, embed), lambda i: (i, 0, 0)),
        name="cell_queries",
    )(cells, proj)


def summary_kernel(
    induced_ref,
    cells_ref,
    query_ref,
    back_ref,
    row_ref,
    summary_ref,
    spread_ref,
    permute_ref,
    o_ref,
    expos_ref,
    point_ref,
    updated_ref,
    values_ref,
    weights_ref,
    total_ref,
):
    step = pl.program_id(0)
    feats, rows, embed = cells_ref.shape
    points = embed
    summaries = total_ref.shape[1] // embed
    ones = jnp.ones((points, embed), jnp.bfloat16)

    @pl.when(step == 0)
    def _():
        expos_ref[...] = jnp.ones_like(expos_ref)
        point_ref[...] = jnp.zeros_like(point_ref)
        updated_ref[...] = jnp.zeros_like(updated_ref)
        values_ref[...] = jnp.zeros_like(values_ref)
        weights_ref[...] = jnp.zeros_like(weights_ref)

    @pl.when(step <= 3)
    def _():
        total_ref[...] = jnp.zeros_like(total_ref)

    values = [values_ref[f].astype(jnp.float32) for f in range(feats)]
    weights = weights_ref[...].astype(jnp.float32)
    for c in range(summaries):
        span = slice(c * embed, (c + 1) * embed)
        if c < 2:
            total_ref[:, span] += (
                weights[:, c : c + 1] * values[0]
                + weights[:, summaries + c : summaries + c + 1] * values[1]
            )
        else:
            wide = product(weights_ref[...], spread_ref[:, 2 * c * embed : 2 * (c + 1) * embed])
            total_ref[:, span] += wide[:, :embed] * values[0] + wide[:, embed:] * values[1]
    row_kv = [product(updated_ref[f], row_ref[...]).astype(jnp.bfloat16) for f in range(feats)]
    for f in range(feats):
        values_ref[f] = row_kv[f][:, embed:]
    keys = jnp.concatenate([row_kv[0][:, :embed], row_kv[1][:, :embed]], axis=1)
    wide = keys.astype(jnp.float32)
    squares = product((wide * wide).astype(jnp.bfloat16), summary_ref[:, embed:])
    factor = lax.rsqrt(squares * (1.0 / embed) + epsilon) * (score_scale * LOG2E)
    scores = product(keys, summary_ref[:, :embed]) * factor
    weights_ref[...] = jnp.exp2(scores).astype(jnp.bfloat16)
    for f in range(feats):
        mixed = product(expos_ref[f], jnp.concatenate([point_ref[f], ones], axis=1))
        attended = mixed[:, :embed] / mixed[:, embed:]
        updated_ref[f] = (cells_ref[f].astype(jnp.float32) + attended).astype(jnp.bfloat16)
    point_kv = product(induced_ref[0, : feats * points, :], back_ref[...]).astype(jnp.bfloat16)
    point_keys = (rms_normalize(point_kv[:, :embed]) * (score_scale * LOG2E)).astype(jnp.bfloat16)
    none = jnp.zeros((points, embed), jnp.bfloat16)
    point_keys = jnp.concatenate(
        [
            jnp.concatenate([point_keys[:points], none], axis=1),
            jnp.concatenate([none, point_keys[points:]], axis=1),
        ],
        axis=0,
    )
    queries = jnp.concatenate([query_ref[f] for f in range(feats)], axis=1)
    expos = jnp.exp2(product_nt(queries, point_keys)).astype(jnp.bfloat16)
    for f in range(feats):
        point_ref[f] = point_kv[f * points : (f + 1) * points, embed:]
        expos_ref[f] = expos[:, f * points : (f + 1) * points]

    @pl.when(step == pl.num_programs(0) - 1)
    def _():
        o_ref[...] = product(permute_ref[...], total_ref[...].astype(jnp.bfloat16)).astype(
            jnp.bfloat16
        )


def summarize(induced, cells, queries, back, row_proj, summary, permute, summaries, pair=2):
    feats, rows, embed = cells.shape
    width = summaries * embed
    steps = feats // pair
    lane = jnp.arange(embed)
    owner = lane // summaries
    scored = [jnp.where(owner[None] == f, jnp.tile(summary, (1, embed // summaries)), 0) for f in range(pair)]
    squared = [jnp.broadcast_to(owner[None] == f, (embed, embed)) for f in range(pair)]
    both = jnp.concatenate(
        [jnp.concatenate(scored, axis=0), jnp.concatenate(squared, axis=0).astype(jnp.bfloat16)],
        axis=1,
    )
    source = jnp.arange(summaries * pair)
    source = (source % pair) * summaries + source // pair
    spread = (lane[:, None] == jnp.repeat(source, embed)[None]).astype(jnp.bfloat16)
    return pl.pallas_call(
        summary_kernel,
        out_shape=jax.ShapeDtypeStruct((rows, width), jnp.bfloat16),
        grid=(steps + 3,),
        in_specs=[
            pl.BlockSpec((1,) + induced.shape[1:], lambda i: (jnp.minimum(i, steps - 1), 0, 0)),
            pl.BlockSpec((pair, rows, embed), lambda i: (jnp.clip(i - 1, 0, steps - 1), 0, 0)),
            pl.BlockSpec((pair, rows, embed), lambda i: (jnp.minimum(i, steps - 1), 0, 0)),
            pl.BlockSpec(back.shape, lambda i: (0, 0)),
            pl.BlockSpec(row_proj.shape, lambda i: (0, 0)),
            pl.BlockSpec(both.shape, lambda i: (0, 0)),
            pl.BlockSpec(spread.shape, lambda i: (0, 0)),
            pl.BlockSpec(permute.shape, lambda i: (0, 0)),
        ],
        out_specs=pl.BlockSpec((rows, width), lambda i: (0, 0)),
        scratch_shapes=[
            pltpu.VMEM((pair, rows, embed), jnp.bfloat16),
            pltpu.VMEM((pair, embed, embed), jnp.bfloat16),
            pltpu.VMEM((pair, rows, embed), jnp.bfloat16),
            pltpu.VMEM((pair, rows, embed), jnp.bfloat16),
            pltpu.VMEM((rows, embed), jnp.bfloat16),
            pltpu.VMEM((rows, width), jnp.float32),
        ],
        name="summarize",
    )(induced, cells, queries, back, row_proj, both, spread, permute)


def attention_kernel(q_ref, qm_ref, kv_ref, km_ref, o_ref, *, groups):
    q = jnp.concatenate([q_ref[...], qm_ref[...]], axis=1)
    count, both, dim = kv_ref.shape
    half = both // 2
    total = jnp.zeros(o_ref.shape, jnp.float32)
    for g in range(0, count, groups):
        k = jnp.concatenate(
            [
                kv_ref[g : g + groups, :half, :].reshape(groups * half, dim),
                km_ref[g * half : (g + groups) * half, :],
            ],
            axis=1,
        )
        v = kv_ref[g : g + groups, half:, :].reshape(groups * half, dim)
        weights = jnp.exp2(product_nt(q, k)).astype(jnp.bfloat16)
        total = total + product(weights, v)
    o_ref[...] = total.astype(o_ref.dtype)


def attention(q, q_marks, kv, k_marks, query_block=1024, groups=8):
    queries, dim = q.shape
    return pl.pallas_call(
        lambda *refs: attention_kernel(*refs, groups=groups),
        out_shape=jax.ShapeDtypeStruct((queries, dim), jnp.bfloat16),
        grid=(queries // query_block,),
        in_specs=[
            pl.BlockSpec((query_block, dim), lambda i: (i, 0)),
            pl.BlockSpec((query_block, dim), lambda i: (i, 0)),
            pl.BlockSpec(kv.shape, lambda i: (0, 0, 0)),
            pl.BlockSpec(k_marks.shape, lambda i: (0, 0)),
        ],
        out_specs=pl.BlockSpec((query_block, dim), lambda i: (i, 0)),
        name="attention",
    )(q, q_marks, kv, k_marks)

def exchange(value, axes):
    return lax.all_to_all(value, axes, 0, 0, tiled=True)


def other(value, axis):
    return lax.ppermute(value, axis, [(0, 1), (1, 0)])


def local(
    table_cells,
    fold_id,
    train_mask,
    inducing,
    induce_proj,
    induce_back,
    summary_query,
    row_proj,
    context_proj,
):
    rows_here, feats_here, embed = table_cells.shape
    width = context_proj.shape[1]
    zl = lax.axis_index("zl")
    core = lax.axis_index("core")
    zh = lax.axis_index("zh")
    xy = lax.axis_index("x") * lax.axis_size("y") + lax.axis_index("y")
    groups_xy = lax.axis_size("x") * lax.axis_size("y")
    groups_z = lax.axis_size("zh")
    feat_devices = lax.axis_size("zl") * lax.axis_size("core")
    block = rows_here // feat_devices
    half = block // 2

    proj_full = jnp.concatenate(
        [
            context_proj,
            other(context_proj, "core"),
            other(context_proj, "zl"),
            lax.ppermute(context_proj, FEAT, [(i, 3 - i) for i in range(4)]),
        ],
        axis=2,
    )

    labelled = (train_mask == 1).astype(jnp.bfloat16)
    index = jnp.arange(rows_here)
    before = (index[:, None] < index[None, :]).astype(jnp.bfloat16)
    rank_train = jnp.dot(labelled[None], before, preferred_element_type=jnp.float32)[0].astype(
        jnp.int32
    )
    rank = jnp.where(train_mask == 1, rank_train, index - rank_train)
    slot = (rank // half) * block + rank % half + jnp.where(train_mask == 1, 0, half)
    permute = (index[:, None] == slot[None, :]).astype(jnp.bfloat16)
    codes = jnp.dot(
        permute, fold_id.astype(jnp.bfloat16)[:, None], preferred_element_type=jnp.float32
    ).astype(jnp.bfloat16)
    codes = codes.reshape(feat_devices, block)

    induce_norm = rms_normalize(inducing).astype(jnp.bfloat16)
    bias = jnp.broadcast_to(
        jnp.where(train_mask == 1, 0.0, EXCLUDED)[None], (8, rows_here)
    ).astype(jnp.float32)
    cells, numerator = induce(table_cells, bias, induce_proj, induce_norm)
    points = inducing.shape[0]
    share_xy = feats_here * points // groups_xy
    numerator, proj_full = lax.optimization_barrier((numerator, proj_full))
    part = exchange(numerator.reshape(groups_xy, share_xy, embed), XY)
    part = jnp.sum(part.astype(jnp.float32), axis=0).astype(jnp.bfloat16)
    queries = cell_queries(cells, induce_back[:, :embed])
    sent = jnp.concatenate([part, jnp.pad(codes, ((0, 12), (0, 0)))], axis=0)
    got = exchange(jnp.broadcast_to(sent[None], (groups_z,) + sent.shape), "zh")
    mine = rms_normalize(jnp.sum(got[:, :share_xy].astype(jnp.float32), axis=0))
    sent = jnp.concatenate(
        [mine.astype(jnp.bfloat16), got[:, share_xy : share_xy + 4].reshape(-1, embed)], axis=0
    )
    got = exchange(jnp.broadcast_to(sent[None], (groups_xy,) + sent.shape), XY)
    all_codes = got[:, share_xy:].reshape(groups_xy, groups_z, feat_devices, block)

    summary = rms_normalize(summary_query).astype(jnp.bfloat16).T
    summaries = summary.shape[1]
    ordered = summarize(
        got, cells, queries, induce_back[:, embed:], row_proj, summary, permute, summaries
    )
    got = exchange(ordered.reshape(feat_devices, block, width), FEAT)
    totals = jnp.sum(got.astype(jnp.float32), axis=0)
    represent = rms_normalize(totals.reshape(block, -1, embed)).astype(jnp.bfloat16)
    projected = jnp.einsum(
        "rd,kdc->krc",
        represent.reshape(block, width),
        proj_full,
        preferred_element_type=jnp.float32,
    ).astype(jnp.bfloat16)

    def placed(value):
        value = jnp.where(zl == 0, value, value[::-1])
        return jnp.where(core == 0, value, value[:, ::-1])

    def heads(value):
        value = value.reshape(-1, 2, 2, HEAD_DIM).transpose(1, 2, 0, 3)
        return placed(value).reshape(feat_devices, -1, HEAD_DIM)

    k = rms_normalize(heads(projected[1][:half])).astype(jnp.bfloat16)
    v = heads(projected[2][:half])
    kv = jnp.concatenate([k, v], axis=1)
    kv_all = exchange(
        jnp.broadcast_to(kv[None], (groups_xy,) + kv.shape).reshape(-1, 2 * half, HEAD_DIM),
        KEY_GROUP,
    )
    q = rms_normalize(projected[0].reshape(block, feat_devices, HEAD_DIM))
    q = (q * (score_scale * LOG2E)).astype(jnp.bfloat16).transpose(1, 0, 2)
    q = q.reshape(2, 2, block, HEAD_DIM)
    q = jnp.stack([q[:, 0], other(q[:, 1], "core")], axis=1)
    q = placed(jnp.stack([q[0], other(q[1], "zl")], axis=0)).reshape(rows_here, HEAD_DIM)
    shifted = [q] + [
        lax.ppermute(q, "zh", [(i, (i + k) % groups_z) for i in range(groups_z)])
        for k in range(1, groups_z)
    ]
    shifted = jnp.stack(shifted[::-1] + shifted[:0:-1])
    q_all = lax.dynamic_slice_in_dim(shifted, groups_z - 1 - zh, groups_z, 0)
    q_all = q_all.reshape(-1, HEAD_DIM)
    query_codes = lax.dynamic_index_in_dim(all_codes, xy, 0, keepdims=False).reshape(-1)
    key_codes = lax.dynamic_index_in_dim(all_codes, zh, 1, keepdims=False)[..., :half].reshape(-1)
    lanes = jnp.arange(HEAD_DIM).astype(jnp.float32)
    query_marks = jnp.where(
        query_codes.astype(jnp.float32)[:, None] == lanes[None], -FOLD_PENALTY, 0.0
    ).astype(jnp.bfloat16)
    key_marks = (key_codes.astype(jnp.float32)[:, None] == lanes[None]).astype(jnp.bfloat16)
    summed = attention(q_all, query_marks, kv_all, key_marks)
    got = exchange(summed.reshape(groups_z, rows_here, HEAD_DIM), "zh")
    context = rms_normalize(jnp.sum(got.astype(jnp.float32), axis=0)).astype(jnp.bfloat16)
    return lax.dot_general(
        permute, context, (((0,), (0,)), ((), ())), preferred_element_type=jnp.float32
    ).astype(jnp.bfloat16)


def solution(mesh):
    fine = Mesh(mesh.devices.reshape(4, 4, 4, 2, 2), ("x", "zh", "y", "zl", "core"))
    rows = ("x", "zh", "y")
    in_specs = (
        P(rows, FEAT, None),
        P(rows),
        P(rows),
        P(),
        P(),
        P(),
        P(),
        P(),
        P(None, None, FEAT),
    )
    return jax.shard_map(
        local, mesh=fine, in_specs=in_specs, out_specs=P(rows, FEAT), check_vma=False
    )
```
